32 devices in a mesh: groups: 2 (over y), strip: 4 (over z), cand: 2 (over x), feat: 2 (over core).
Axes of the slice: x: 2, y: 2, z: 4, core: 2. Of those that a mesh axis runs over, the one named last changes fastest.
Arguments:
- src_pos: float32 [3, 32768], P(None, ('groups', 'strip')), parts along dimension 1, may hold values from -1 to 1
- src_feat: bfloat16 [128, 32768], P('feat', ('groups', 'strip')), parts along dimension 1, may hold values from -10.5 to 10.5
- tgt_pos: float32 [3, 32768], P(None, ('groups', 'strip', 'cand')), parts along dimension 1, may hold values from -0.6 to 1.4
- tgt_feat: bfloat16 [128, 32768], P('feat', ('groups', 'strip', 'cand')), parts along dimension 1, may hold values from -10.5 to 10.5
- displacement: float32 [3, 32768], P(None, ('groups', 'strip')), parts along dimension 1, may hold values from -1 to 1
- sigma_sq: float32 [8], P(('groups', 'strip')), parts along dimension 0, may hold values from 0.5 to 2
- seed_target: int32 [32768], P(('groups', 'strip')), parts along dimension 0, may hold values from 0 to 8191
- counts: int32 [8], P(('groups', 'strip')), parts along dimension 0, may hold values from 512 to 4096
- edges: int32 [8, 32768], P(None, ('groups', 'strip')), parts along dimension 1, may hold values from 0 to 12287, as said below
Outputs:
- new_disp: float32 [3, 32768], P(None, ('groups', 'strip')), parts along dimension 1
- match_mass: float32 [32768], P(('groups', 'strip')), parts along dimension 0
The draws below stay inside these ranges and needn't reach their ends.
There are 2 independent parts, one for each index of `groups`. The reference program is written for one: setup_inputs(seed, part) draws one part's arguments, and reference() takes and returns one part's arrays. A program takes and returns all parts, laid end to end along the dimension named above; each array names one. Nothing has to cross between parts.
Inputs may be any that keep to these rules, and one draw needn't show every extreme that they name: `seed_target`: values of 4096 or more mean that the point has no tie point. `edges`: the strip that an edge names exists, and its slot is below that strip's count; for a live source point at slot i the slot that an edge names lies within 16 of i.
All inputs are finite; a program needn't handle non-finite values.
Results may differ from the reference program's by a relative error of at most 0.0003.
Values may be sent and summed in bfloat16 or wider, within the bound.
A program may use at most 128 MiB of HBM per device.

```python
import math
import jax
import jax.numpy as jnp
from jax import lax

FEAT = 128
POINTS_DEV = 4096
NEIGHBOURS = 8
REACH = 16
SWEEPS = 4
CAND = 4096
POINTS = 16384
TARGETS = 16384
N_STRIP = 4


def draw_src_feat(key, part):
    base = jnp.clip(jax.random.normal(jax.random.fold_in(key, 1), (FEAT, N_STRIP, POINTS_DEV), jnp.float32), -4.0, 4.0)
    return base.reshape(FEAT, POINTS).astype(jnp.bfloat16)


def draw_tgt_feat(key, part):
    base = jnp.clip(jax.random.normal(jax.random.fold_in(key, 2), (FEAT, N_STRIP, CAND), jnp.float32), -4.0, 4.0)
    return base.reshape(FEAT, TARGETS).astype(jnp.bfloat16)


def strip_layout(key):
    lowest = max(1, POINTS_DEV // 8)
    base = jax.random.randint(jax.random.fold_in(key, 21), (N_STRIP,), lowest, POINTS_DEV + 1, dtype=jnp.int32)
    fullest = jax.random.randint(jax.random.fold_in(key, 22), (), 1, N_STRIP, dtype=jnp.int32)
    step_away = jax.random.randint(jax.random.fold_in(key, 23), (), 1, N_STRIP, dtype=jnp.int32)
    lightest = (fullest + step_away) % N_STRIP
    base = base.at[fullest].set(POINTS_DEV)
    base = base.at[lightest].set(lowest)
    return (base, fullest)


def draw_counts(key, part):
    layout, fullest = strip_layout(key)
    return layout


def draw_edges(key, part):
    layout, fullest = strip_layout(key)
    shape = (NEIGHBOURS, N_STRIP, POINTS_DEV)
    strip_ids = jnp.arange(N_STRIP, dtype=jnp.int32)[None, :, None]
    slot_ids = jnp.arange(POINTS_DEV, dtype=jnp.int32)[None, None, :]
    pick = jax.random.randint(jax.random.fold_in(key, 24), shape, 0, 4, dtype=jnp.int32)
    segment = pick - (pick >= 2).astype(jnp.int32)
    target_strip = strip_ids + segment - 1
    outside = (target_strip < 0) | (target_strip >= N_STRIP)
    segment = jnp.where(outside, 1, segment)
    target_strip = strip_ids + segment - 1
    room = jnp.take(layout, target_strip)
    own = jnp.take(layout, strip_ids)
    delta = jax.random.randint(jax.random.fold_in(key, 26), shape, -REACH, REACH + 1, dtype=jnp.int32)
    wanted = slot_ids + delta
    inside = (wanted >= 0) & (wanted < room)
    fallback = jnp.clip(wanted, 0, own - 1)
    raw = jax.random.randint(jax.random.fold_in(key, 25), shape, 0, 1 << 20, dtype=jnp.int32)
    live_source = slot_ids < own
    slot = jnp.where(live_source, jnp.where(inside, wanted, fallback), raw % room)
    segment = jnp.where(live_source & jnp.logical_not(inside), 1, segment)
    values = segment * POINTS_DEV + slot
    values = values.at[0, 1, 0].set(0)
    values = values.at[1, fullest - 1, POINTS_DEV - 1].set(3 * POINTS_DEV - 1)
    return values.reshape(NEIGHBOURS, POINTS).astype(jnp.int32)


def plant(values, key, smallest, top_value):
    longest = values.shape.index(max(values.shape))
    spots = []
    for shift in (0, 1):
        where = [jax.random.randint(jax.random.fold_in(key, axis), (), 0, length) for axis, length in enumerate(values.shape)]
        where[longest] = (where[longest] + shift) % values.shape[longest]
        spots.append(tuple(where))
    return values.at[spots[0]].set(smallest).at[spots[1]].set(top_value)


def level_of(key, extent, shards, least, largest):
    def one(axis_at, parts):
        heights = jax.random.uniform(jax.random.fold_in(jax.random.fold_in(key, 6), axis_at), (parts,), jnp.float32, least / len(shards), largest / len(shards))
        return jnp.repeat(jnp.exp(heights), extent[axis_at] // parts).reshape((-1,) + (1,) * (len(extent) - axis_at - 1))

    factor_of = one(*shards[0])
    for cut in shards[1:]:
        factor_of = factor_of * one(*cut)
    return factor_of


def centred(key, shape, deviation, limit, pieces=(), kind=jnp.bfloat16):
    loudness = level_of(key, shape, pieces, -0.22, 0.18) if pieces else 1.0
    result = jax.random.normal(key, shape, jnp.float32) * deviation * loudness
    return jnp.minimum(jnp.maximum(result, -limit), limit).astype(kind)


def setup_inputs(seed: int = 0, part: int = 0) -> dict:
    key_list = jax.random.split(jax.random.key(seed), 10)
    part_keys = jax.random.split(jax.random.fold_in(key_list[9], part), 10)
    src_pos = jnp.clip(jax.random.uniform(part_keys[0], (3, POINTS), jnp.float32, -1.0, 1.0) * level_of(part_keys[0], (3, POINTS), ((1, 4),), -0.4, 0.0), -1.0, 1.0)
    src_feat = draw_src_feat(jax.random.fold_in(jax.random.fold_in(key_list[9], part), 71), part)
    tgt_pos = jnp.clip(-0.6 + 2.0 * jax.random.uniform(part_keys[2], (3, TARGETS), jnp.float32) ** level_of(part_keys[2], (3, TARGETS), ((1, 8),), -0.2, 0.2), -0.6, 1.4)
    tgt_feat = draw_tgt_feat(jax.random.fold_in(jax.random.fold_in(key_list[9], part), 71), part)
    displacement = centred(part_keys[4], (3, POINTS), 0.2, 1.0, ((1, 4),), jnp.float32)
    sigma_sq = jnp.clip(jnp.exp(math.log(2.0) - 1.3862944 * jax.random.uniform(part_keys[5], (N_STRIP,), jnp.float32) ** level_of(part_keys[5], (N_STRIP,), ((0, 4),), -0.2, 0.2)), 0.5, 2.0)
    seed_target = plant(jax.random.randint(part_keys[6], (POINTS,), 0, 2 * CAND), jax.random.fold_in(part_keys[6], 1), 0, (2 * CAND) - 1).astype(jnp.int32)
    counts = draw_counts(jax.random.fold_in(jax.random.fold_in(key_list[9], part), 71), part)
    edges = draw_edges(jax.random.fold_in(jax.random.fold_in(key_list[9], part), 71), part)
    return {"src_pos": src_pos, "src_feat": src_feat, "tgt_pos": tgt_pos, "tgt_feat": tgt_feat, "displacement": displacement, "sigma_sq": sigma_sq, "seed_target": seed_target, "counts": counts, "edges": edges}


feature_scale = 0.18
tie_gain = 3.0
outlier_level = 1.0
strip_offset = 2.0
kernel_scale = 8.0
coherence = 0.1


def strip_posterior(items):
    z_strip, feat_strip, x_strip, tfeat_strip, sigma, seeds = items
    width = min(512, POINTS_DEV)
    count = POINTS_DEV // width
    tfloat = tfeat_strip.astype(jnp.float32)
    columns = jnp.arange(CAND, dtype=jnp.int32)

    def one_block(index):
        begin = (index * width).astype(jnp.int32)
        zblock = lax.dynamic_slice_in_dim(z_strip, begin, width, 1)
        fblock = lax.dynamic_slice_in_dim(feat_strip, begin, width, 1).astype(jnp.float32)
        sblock = lax.dynamic_slice_in_dim(seeds, begin, width, 0)
        product = jnp.dot(fblock.T, tfloat, precision=lax.Precision.HIGHEST)
        dist = (x_strip[0][None, :] - zblock[0][:, None]) ** 2
        dist = dist + (x_strip[1][None, :] - zblock[1][:, None]) ** 2
        dist = dist + (x_strip[2][None, :] - zblock[2][:, None]) ** 2
        match = (columns[None, :] == sblock[:, None]).astype(jnp.float32)
        score = feature_scale * product - dist / (2.0 * sigma) + tie_gain * match
        peak = jnp.maximum(jnp.max(score, axis=1), outlier_level)
        expo = jnp.exp(score - peak[:, None])
        total = jnp.sum(expo, axis=1)
        moment = jnp.dot(x_strip, expo.T, precision=lax.Precision.HIGHEST)
        denom = total + jnp.exp(outlier_level - peak)
        return total / denom, moment / denom[None, :]

    mass, moment = lax.map(one_block, jnp.arange(count, dtype=jnp.int32))
    mass = mass.reshape(POINTS_DEV)
    moment = jnp.transpose(moment, (1, 0, 2)).reshape(3, POINTS_DEV)
    return mass, moment


def reference(src_pos, src_feat, tgt_pos, tgt_feat, displacement, sigma_sq, seed_target, counts, edges):
    strips = N_STRIP
    zpos = src_pos + displacement
    zs = jnp.transpose(zpos.reshape(3, strips, POINTS_DEV), (1, 0, 2))
    ys = jnp.transpose(src_pos.reshape(3, strips, POINTS_DEV), (1, 0, 2))
    vs = jnp.transpose(displacement.reshape(3, strips, POINTS_DEV), (1, 0, 2))
    fs = jnp.transpose(src_feat.reshape(FEAT, strips, POINTS_DEV), (1, 0, 2))
    xs = jnp.transpose(tgt_pos.reshape(3, strips, CAND), (1, 0, 2))
    txs = jnp.transpose(tgt_feat.reshape(FEAT, strips, CAND), (1, 0, 2))
    seeds = seed_target.reshape(strips, POINTS_DEV)
    mass, moment = lax.map(strip_posterior, (zs, fs, xs, txs, sigma_sq, seeds))
    slots = jnp.arange(POINTS_DEV, dtype=jnp.int32)
    live = (slots[None, :] < counts[:, None]).astype(jnp.float32)
    mass = mass * live
    moment = moment * live[:, None, :]
    resid = moment - mass[:, None, :] * zs
    geometry = jnp.concatenate([ys, live[:, None, :]], axis=1)
    padded = jnp.pad(geometry, ((1, 1), (0, 0), (0, 0)))
    flat_geo = jnp.transpose(padded, (1, 0, 2)).reshape(4, (strips + 2) * POINTS_DEV)
    edge = jnp.transpose(edges.reshape(NEIGHBOURS, strips, POINTS_DEV), (1, 0, 2))
    segment = edge // POINTS_DEV
    local = edge % POINTS_DEV
    strip_ids = jnp.arange(strips, dtype=jnp.int32)
    flat = ((strip_ids[:, None, None] + segment) * POINTS_DEV + local).astype(jnp.int32)
    neigh = flat_geo[:, flat]
    shift = strip_offset * (segment - 1).astype(jnp.float32)
    d0 = ys[:, 0][:, None, :] - neigh[0] - shift
    d1 = ys[:, 1][:, None, :] - neigh[1]
    d2 = ys[:, 2][:, None, :] - neigh[2]
    kernel = live[:, None, :] * neigh[3] * jnp.exp(-(d0 * d0 + d1 * d1 + d2 * d2) / (2.0 * kernel_scale)) / NEIGHBOURS

    def spread(field):
        fpad = jnp.pad(field, ((1, 1), (0, 0), (0, 0)))
        fflat = jnp.transpose(fpad, (1, 0, 2)).reshape(3, (strips + 2) * POINTS_DEV)
        got = fflat[:, flat]
        return jnp.transpose(jnp.sum(kernel[None] * got, axis=2), (1, 0, 2))

    diag = mass + coherence * sigma_sq[:, None]
    field = resid / diag[:, None, :]
    for sweep in range(SWEEPS):
        field = (resid - mass[:, None, :] * spread(field)) / diag[:, None, :]
    new_disp = vs + field + spread(field)
    new_disp = jnp.transpose(new_disp, (1, 0, 2)).reshape(3, POINTS)
    return new_disp, mass.reshape(POINTS)
```

```python
import math

import jax
import jax.numpy as jnp
from jax import lax
from jax.experimental import pallas as pl
from jax.experimental.pallas import tpu as pltpu
from jax.sharding import PartitionSpec as P

SWEEPS = 4
LANES = 128
BLOCK = 256

feature_scale = 0.18
tie_gain = 3.0
outlier_level = 1.0
strip_offset = 2.0
kernel_scale = 8.0
coherence = 0.1

EXP2 = feature_scale * math.log2(math.e)
FLOOR = outlier_level / feature_scale
MESH = pl.DeviceIdType.MESH


def split3(value):
    high = value.astype(jnp.bfloat16).astype(jnp.float32)
    rest = value - high
    mid = rest.astype(jnp.bfloat16).astype(jnp.float32)
    return high, mid, rest - mid


def rows8(rows, width):
    at = lax.broadcasted_iota(jnp.int32, (8, width), 0)
    out = jnp.zeros((8, width), jnp.float32)
    for i, row in enumerate(rows):
        out = jnp.where(at == i, jnp.broadcast_to(row, (8, width)), out)
    return out


def posterior_kernel(
    sigma_ref, src_feat, tgt_feat, src_pos, disp, tgt_pos, seed, out,
    sfeat, tmat, saug, xmat, send_sem, recv_sem,
):
    chans, points = src_feat.shape
    cands = tgt_feat.shape[1]
    half = points // 2
    me = lax.axis_index("feat")
    other = 1 - me
    offset = lax.axis_index("cand") * cands
    barrier = pltpu.get_barrier_semaphore()
    pl.semaphore_signal(barrier, inc=1, device_id={"feat": other}, device_id_type=MESH)
    pl.semaphore_wait(barrier, 1)
    theirs = pl.ds(pl.multiple_of(other * half, LANES), half)
    mine = pl.ds(pl.multiple_of(me * half, LANES), half)
    copies = [
        pltpu.make_async_remote_copy(
            src_ref=tgt_feat, dst_ref=tmat.at[pl.ds(chans, chans)],
            send_sem=send_sem.at[0], recv_sem=recv_sem.at[0],
            device_id={"feat": other}, device_id_type=MESH,
        ),
        pltpu.make_async_remote_copy(
            src_ref=src_feat.at[:, theirs], dst_ref=sfeat.at[pl.ds(chans, chans)],
            send_sem=send_sem.at[1], recv_sem=recv_sem.at[1],
            device_id={"feat": other}, device_id_type=MESH,
        ),
    ]
    for copy in copies:
        copy.start()
    tmat[0:chans] = tgt_feat[...]
    sfeat[0:chans] = src_feat[:, mine]
    inv = 1.0 / (sigma_ref[0, 0] * feature_scale)
    x = [tgt_pos[i : i + 1, :] for i in range(3)]
    xx = x[0] * x[0] + x[1] * x[1] + x[2] * x[2]
    one = jnp.ones((1, cands), jnp.float32)
    high, mid, low = split3(rows8(x + [xx * (-0.5 * inv), one], cands))
    tmat[2 * chans : 2 * chans + 48] = jnp.concatenate(
        [high, high, mid, mid, high, low], axis=0
    ).astype(jnp.bfloat16)
    high, mid, low = split3(rows8(x + [one], cands))
    columns = jnp.concatenate(
        [high, mid, low, jnp.zeros((LANES - 24, cands), jnp.float32)], axis=0
    )
    xmat[...] = jnp.transpose(columns).astype(jnp.bfloat16)
    z = [src_pos[i : i + 1, mine] + disp[i : i + 1, mine] for i in range(3)]
    zz = z[0] * z[0] + z[1] * z[1] + z[2] * z[2]
    ones = jnp.ones((1, half), jnp.float32)
    high, mid, low = split3(rows8([v * inv for v in z] + [ones, zz * (-0.5 * inv)], half))
    saug[...] = jnp.concatenate([high, mid, high, mid, low, high], axis=0).astype(jnp.bfloat16)
    for copy in copies:
        copy.wait()

    def block(index, carry):
        span = pl.ds(pl.multiple_of(index * BLOCK, BLOCK), BLOCK)
        lhs = jnp.concatenate([sfeat[:, span], saug[:, span]], axis=0)
        score = lax.dot_general(
            lhs, tmat[...], (((0,), (0,)), ((), ())), preferred_element_type=jnp.float32
        )
        seeds = []
        for i in range(BLOCK // LANES):
            row = seed[pl.ds(me * (half // LANES) + index * (BLOCK // LANES) + i, 1), :] - offset
            seeds.append(jnp.transpose(jnp.broadcast_to(row.astype(jnp.float32), (LANES, LANES))))
        seeds = jnp.concatenate(seeds, axis=0)
        lane = lax.broadcasted_iota(jnp.int32, (BLOCK, LANES), 1).astype(jnp.float32)
        pieces = []
        for t in range(cands // LANES):
            piece = score[:, t * LANES : (t + 1) * LANES]
            tie = jnp.where(seeds == lane + float(t * LANES), tie_gain / feature_scale, 0.0)
            pieces.append(piece + tie)
        best = pieces[0]
        for piece in pieces[1:]:
            best = jnp.maximum(best, piece)
        peak = jnp.maximum(jnp.max(best, axis=1, keepdims=True), FLOOR)
        weight = jnp.concatenate([jnp.exp2((piece - peak) * EXP2) for piece in pieces], axis=1)
        high = weight.astype(jnp.bfloat16)
        low = (weight - high.astype(jnp.float32)).astype(jnp.bfloat16)
        sums = jnp.dot(high, xmat[...], preferred_element_type=jnp.float32)
        sums = sums + jnp.dot(low, xmat[...], preferred_element_type=jnp.float32)
        at = lax.broadcasted_iota(jnp.int32, (BLOCK, LANES), 1)
        sums = jnp.where(at == 28, jnp.broadcast_to(peak, (BLOCK, LANES)), sums)
        for i in range(BLOCK // LANES):
            turned = jnp.transpose(sums[i * LANES : (i + 1) * LANES])
            out[index * (BLOCK // LANES) + i] = (
                turned[0:8] + turned[8:16] + turned[16:24] + turned[24:32]
            )
        return carry

    lax.fori_loop(0, half // BLOCK, block, 0)


def sweep_kernel(
    sigma_ref, count_ref, part, src_pos, disp, edges, new_disp, mass_out,
    parts, pos, dis, edge, geo, geo_in, where_at, kern_own, kern_far, field, field_in,
    resid, mass_s, part_send, part_recv, geo_send, geo_recv, field_send, field_recv,
):
    points = src_pos.shape[1]
    tiles = points // LANES
    cand_n, strip_n = lax.axis_size("cand"), lax.axis_size("strip")
    s, c, f = lax.axis_index("strip"), lax.axis_index("cand"), lax.axis_index("feat")
    below, above = s > 0, s < strip_n - 1
    barrier = pltpu.get_barrier_semaphore()
    peers = [(dc, df) for dc in range(cand_n) for df in range(2) if dc or df]

    def peer(dc, df):
        return {"cand": lax.rem(c + dc, cand_n), "feat": lax.rem(f + df, 2)}

    for dc, df in peers:
        pl.semaphore_signal(barrier, inc=1, device_id=peer(dc, df), device_id_type=MESH)

    @pl.when(below)
    def _():
        pl.semaphore_signal(barrier, inc=1, device_id={"strip": s - 1}, device_id_type=MESH)

    @pl.when(above)
    def _():
        pl.semaphore_signal(barrier, inc=1, device_id={"strip": s + 1}, device_id_type=MESH)

    slot = (
        lax.broadcasted_iota(jnp.int32, (tiles, LANES), 0) * LANES
        + lax.broadcasted_iota(jnp.int32, (tiles, LANES), 1)
    )
    live = (slot < count_ref[0, 0]).astype(jnp.float32)
    for t in range(tiles):
        span = slice(t * LANES, (t + 1) * LANES)
        geo[0:3, t, :] = src_pos[:, span]
        dis[:, t, :] = disp[:, span]
        edge[:, t, :] = edges[:, span]
    geo[3] = live
    parts[0, c] = part[...]

    pl.semaphore_wait(barrier, len(peers) + below.astype(jnp.int32) + above.astype(jnp.int32))

    part_copies = []
    for i, (dc, df) in enumerate(peers):
        copy = pltpu.make_async_remote_copy(
            src_ref=part, dst_ref=parts.at[df, c],
            send_sem=part_send.at[i], recv_sem=part_recv.at[i],
            device_id=peer(dc, df), device_id_type=MESH,
        )
        copy.start()
        part_copies.append(copy)

    def beside(src, dst, send, recv):
        down = pltpu.make_async_remote_copy(
            src_ref=src, dst_ref=dst.at[1], send_sem=send.at[0], recv_sem=recv.at[1],
            device_id={"strip": jnp.maximum(s - 1, 0)}, device_id_type=MESH,
        )
        up = pltpu.make_async_remote_copy(
            src_ref=src, dst_ref=dst.at[0], send_sem=send.at[1], recv_sem=recv.at[0],
            device_id={"strip": jnp.minimum(s + 1, strip_n - 1)}, device_id_type=MESH,
        )

        @pl.when(below)
        def _():
            down.start()

        @pl.when(above)
        def _():
            up.start()

        def finish():
            @pl.when(below)
            def _():
                down.wait_send()
                up.wait_recv()

            @pl.when(above)
            def _():
                up.wait_send()
                down.wait_recv()

        return finish

    @pl.when(jnp.logical_not(below))
    def _():
        geo_in[0] = jnp.zeros(geo_in.shape[1:], jnp.float32)
        for k in range(SWEEPS + 1):
            field_in[k, 0] = jnp.zeros(field_in.shape[2:], jnp.float32)

    @pl.when(jnp.logical_not(above))
    def _():
        geo_in[1] = jnp.zeros(geo_in.shape[1:], jnp.float32)
        for k in range(SWEEPS + 1):
            field_in[k, 1] = jnp.zeros(field_in.shape[2:], jnp.float32)

    finish_geo = beside(geo, geo_in, geo_send, geo_recv)
    lane = lax.broadcasted_iota(jnp.int32, (tiles, LANES), 1)
    row = lax.broadcasted_iota(jnp.int32, (tiles, LANES), 0)

    def pair(array):
        ends = jnp.where(lane < LANES // 2, pltpu.roll(array, tiles - 1, 0), pltpu.roll(array, 1, 0))
        return array, ends

    def pick(arrays, at, inside):
        return jnp.where(
            inside,
            jnp.take_along_axis(arrays[0], at, axis=1, mode="promise_in_bounds"),
            jnp.take_along_axis(arrays[1], at, axis=1, mode="promise_in_bounds"),
        )

    def decode(k):
        e = edge[k]
        segment = (e >= points).astype(jnp.int32) + (e >= 2 * points).astype(jnp.int32)
        local = e - segment * points
        return segment, lax.bitwise_and(local, LANES - 1), lax.shift_right_logical(local, 7) == row

    finish_geo()
    sources = [
        [pair(geo_in[0, i]), pair(geo[i]), pair(geo_in[1, i])] for i in range(4)
    ]
    for k in range(edges.shape[0]):
        segment, at, inside = decode(k)
        near = [
            jnp.where(
                segment == 1,
                pick(three[1], at, inside),
                jnp.where(segment == 0, pick(three[0], at, inside), pick(three[2], at, inside)),
            )
            for three in sources
        ]
        d0 = geo[0] - near[0] - strip_offset * (segment - 1).astype(jnp.float32)
        d1 = geo[1] - near[1]
        d2 = geo[2] - near[2]
        squared = d0 * d0 + d1 * d1 + d2 * d2
        value = live * near[3] * jnp.exp(squared * (-0.5 / kernel_scale)) / edges.shape[0]
        value = jnp.where(slot < count_ref[0, 0], value, 0.0)
        kern_own[k] = jnp.where(segment == 1, value, 0.0)
        kern_far[k] = jnp.where(segment == 1, 0.0, value)

    for copy in part_copies:
        copy.wait()
    rows = tiles // 2
    sigma = sigma_ref[0, 0]
    for df in range(2):
        half_at = lax.rem(f + df, 2) * rows
        span = pl.ds(pl.multiple_of(half_at, 8), rows)
        peaks = [parts[df, i, :, 4, :] for i in range(cand_n)]
        peak = peaks[0]
        for other in peaks[1:]:
            peak = jnp.maximum(peak, other)
        sums = [jnp.zeros((rows, LANES), jnp.float32) for _ in range(4)]
        for i in range(cand_n):
            scale = jnp.exp2((peaks[i] - peak) * EXP2)
            sums = [sums[j] + parts[df, i, :, j, :] * scale for j in range(4)]
        denom = sums[3] + jnp.exp2((FLOOR - peak) * EXP2)
        at = lax.broadcasted_iota(jnp.int32, (rows, LANES), 0) * LANES + lax.broadcasted_iota(
            jnp.int32, (rows, LANES), 1
        )
        on = (at + half_at * LANES < count_ref[0, 0]).astype(jnp.float32)
        share = on / denom
        mass = sums[3] * share
        mass_s[span] = mass
        for j in range(3):
            resid[j, span] = sums[j] * share - mass * (geo[j, span] + dis[j, span])

    mass = mass_s[...]
    mass_out[...] = mass
    inverse = 1.0 / (mass + coherence * sigma)
    for j in range(3):
        field[0, j] = resid[j] * inverse

    for step in range(SWEEPS + 1):
        finish = beside(field.at[step], field_in.at[step], field_send.at[step], field_recv.at[step])
        own = [pair(field[step, j]) for j in range(3)]
        acc = [jnp.zeros((tiles, LANES), jnp.float32) for _ in range(3)]
        for k in range(edges.shape[0]):
            _, at, inside = decode(k)
            weight = kern_own[k]
            acc = [acc[j] + weight * pick(own[j], at, inside) for j in range(3)]
        finish()
        low = [pair(field_in[step, 0, j]) for j in range(3)]
        high = [pair(field_in[step, 1, j]) for j in range(3)]
        for k in range(edges.shape[0]):
            segment, at, inside = decode(k)
            weight = kern_far[k]
            acc = [
                acc[j]
                + weight
                * jnp.where(segment == 0, pick(low[j], at, inside), pick(high[j], at, inside))
                for j in range(3)
            ]
        if step < SWEEPS:
            for j in range(3):
                field[step + 1, j] = (resid[j] - mass_s[...] * acc[j]) * inverse
        else:
            for j in range(3):
                pos[j] = dis[j] + field[step, j] + acc[j]
    for t in range(tiles):
        new_disp[:, t * LANES : (t + 1) * LANES] = pos[:, t, :]


def on_device(
    src_pos, src_feat, tgt_pos, tgt_feat, displacement, sigma_sq, seed_target, counts, edges
):
    chans, points = src_feat.shape
    cands = tgt_pos.shape[1]
    half = points // 2
    tiles = points // LANES
    edge_n = edges.shape[0]
    cand_n = lax.axis_size("cand")
    sigma = sigma_sq.reshape(1, 1)
    count = counts.reshape(1, 1)
    vmem = pl.BlockSpec(memory_space=pltpu.VMEM)
    smem = pl.BlockSpec(memory_space=pltpu.SMEM)
    f32, bf16 = jnp.float32, jnp.bfloat16
    part = pl.pallas_call(
        posterior_kernel,
        out_shape=jax.ShapeDtypeStruct((half // LANES, 8, LANES), f32),
        in_specs=[smem] + [vmem] * 6,
        out_specs=vmem,
        scratch_shapes=[
            pltpu.VMEM((2 * chans, half), bf16),
            pltpu.VMEM((2 * chans + 48, cands), bf16),
            pltpu.VMEM((48, half), bf16),
            pltpu.VMEM((cands, LANES), bf16),
            pltpu.SemaphoreType.DMA((2,)),
            pltpu.SemaphoreType.DMA((2,)),
        ],
        compiler_params=pltpu.CompilerParams(
            collective_id=0, has_side_effects=True, vmem_limit_bytes=48 << 20
        ),
    )(sigma, src_feat, tgt_feat, src_pos, displacement, tgt_pos, seed_target.reshape(tiles, LANES))
    grid = (tiles, LANES)
    new_disp, mass = pl.pallas_call(
        sweep_kernel,
        out_shape=(
            jax.ShapeDtypeStruct((3, points), f32),
            jax.ShapeDtypeStruct(grid, f32),
        ),
        in_specs=[smem, smem] + [vmem] * 4,
        out_specs=(vmem, vmem),
        scratch_shapes=[
            pltpu.VMEM((2, cand_n, half // LANES, 8, LANES), f32),
            pltpu.VMEM((3,) + grid, f32),
            pltpu.VMEM((3,) + grid, f32),
            pltpu.VMEM((edge_n,) + grid, jnp.int32),
            pltpu.VMEM((4,) + grid, f32),
            pltpu.VMEM((2, 4) + grid, f32),
            pltpu.VMEM((8, LANES), jnp.int32),
            pltpu.VMEM((edge_n,) + grid, f32),
            pltpu.VMEM((edge_n,) + grid, f32),
            pltpu.VMEM((SWEEPS + 1, 3) + grid, f32),
            pltpu.VMEM((SWEEPS + 1, 2, 3) + grid, f32),
            pltpu.VMEM((3,) + grid, f32),
            pltpu.VMEM(grid, f32),
            pltpu.SemaphoreType.DMA((2 * cand_n - 1,)),
            pltpu.SemaphoreType.DMA((2 * cand_n - 1,)),
            pltpu.SemaphoreType.DMA((2,)),
            pltpu.SemaphoreType.DMA((2,)),
            pltpu.SemaphoreType.DMA((SWEEPS + 1, 2)),
            pltpu.SemaphoreType.DMA((SWEEPS + 1, 2)),
        ],
        compiler_params=pltpu.CompilerParams(
            collective_id=1, has_side_effects=True, vmem_limit_bytes=48 << 20
        ),
    )(sigma, count, part, src_pos, displacement, edges)
    return (new_disp, mass.reshape(points))


def solution(mesh):
    in_specs = (
        P(None, ("groups", "strip")),
        P("feat", ("groups", "strip")),
        P(None, ("groups", "strip", "cand")),
        P("feat", ("groups", "strip", "cand")),
        P(None, ("groups", "strip")),
        P(("groups", "strip")),
        P(("groups", "strip")),
        P(("groups", "strip")),
        P(None, ("groups", "strip")),
    )
    out_specs = (P(None, ("groups", "strip")), P(("groups", "strip")))
    return jax.shard_map(
        on_device, mesh=mesh, in_specs=in_specs, out_specs=out_specs, check_vma=False
    )
```

```python
import math

import jax
import jax.numpy as jnp
from jax import lax
from jax.experimental import pallas as pl
from jax.experimental.pallas import tpu as pltpu
from jax.sharding import PartitionSpec as P

SWEEPS = 4
LANES = 128
BLOCK = 256
REACH = 16

feature_scale = 0.18
tie_gain = 3.0
outlier_level = 1.0
strip_offset = 2.0
kernel_scale = 8.0
coherence = 0.1

EXP2 = feature_scale * math.log2(math.e)
FLOOR = outlier_level / feature_scale
MESH = pl.DeviceIdType.MESH


def split3(value):
    high = value.astype(jnp.bfloat16).astype(jnp.float32)
    rest = value - high
    mid = rest.astype(jnp.bfloat16).astype(jnp.float32)
    return high, mid, rest - mid


def rows8(rows, width):
    at = lax.broadcasted_iota(jnp.int32, (8, width), 0)
    out = jnp.zeros((8, width), jnp.float32)
    for i, row in enumerate(rows):
        out = jnp.where(at == i, jnp.broadcast_to(row, (8, width)), out)
    return out


def cpd_kernel(
    sigma_ref, count_ref, src_feat, tgt_feat, src_pos_in, disp_in, tgt_pos_in, seed_in, edges_in,
    new_disp, mass_out,
    src_pos, disp, tgt_pos, seed, edges, sfeat, tmat, saug, xmat, state,
    parts, pos, edge, geo, geo_in, gaps, kern_own, kern_far, field, field_in, resid, mass_s,
    local_sem, feat_send, feat_recv, part_send, part_recv, geo_send, geo_recv,
    field_send, field_recv, out_send, out_recv,
):
    chans, points = src_feat.shape
    cands = tgt_feat.shape[1]
    tiles = points // LANES
    half = points // 2
    half_tiles = tiles // 2
    wide = half + LANES
    cand_n, strip_n = lax.axis_size("cand"), lax.axis_size("strip")
    s, c, f = lax.axis_index("strip"), lax.axis_index("cand"), lax.axis_index("feat")
    other = 1 - f
    below, above = s > 0, s < strip_n - 1
    own_tiles = half_tiles // cand_n
    rows = own_tiles + 2
    stack = field.shape[1]
    edge_n = edges.shape[0]
    sigma = sigma_ref[0, 0]
    count = count_ref[0, 0]

    def wide_of(part):
        return pl.ds(pl.multiple_of(part * (half - LANES), LANES), wide)

    loads = [
        pltpu.make_async_copy(src, dst, local_sem.at[i])
        for i, (src, dst) in enumerate(
            [
                (tgt_pos_in, tgt_pos),
                (src_pos_in, src_pos),
                (disp_in, disp),
                (seed_in, seed),
                (edges_in, edges),
                (tgt_feat, tmat.at[pl.ds(0, chans)]),
                (src_feat.at[:, wide_of(f)], sfeat.at[pl.ds(0, chans)]),
            ]
        )
    ]
    for load in loads:
        load.start()

    barrier = pltpu.get_barrier_semaphore()
    peers = [(dc, df) for dc in range(cand_n) for df in range(2) if dc or df]

    def peer(dc, df):
        return {"cand": lax.rem(c + dc, cand_n), "feat": lax.rem(f + df, 2)}

    for dc, df in peers:
        pl.semaphore_signal(barrier, inc=1, device_id=peer(dc, df), device_id_type=MESH)

    @pl.when(below)
    def _():
        pl.semaphore_signal(barrier, inc=1, device_id={"strip": s - 1}, device_id_type=MESH)

    @pl.when(above)
    def _():
        pl.semaphore_signal(barrier, inc=1, device_id={"strip": s + 1}, device_id_type=MESH)

    pl.semaphore_wait(barrier, len(peers) + below.astype(jnp.int32) + above.astype(jnp.int32))

    feats = [
        pltpu.make_async_remote_copy(
            src_ref=src, dst_ref=dst, send_sem=feat_send.at[i], recv_sem=feat_recv.at[i],
            device_id={"feat": other}, device_id_type=MESH,
        )
        for i, (src, dst) in enumerate(
            [
                (tgt_feat, tmat.at[pl.ds(chans, chans)]),
                (src_feat.at[:, wide_of(other)], sfeat.at[pl.ds(chans, chans)]),
            ]
        )
    ]
    for copy in feats:
        copy.start()

    def beside(src, dst, send, recv):
        down = pltpu.make_async_remote_copy(
            src_ref=src, dst_ref=dst.at[1], send_sem=send.at[0], recv_sem=recv.at[1],
            device_id={"strip": jnp.maximum(s - 1, 0)}, device_id_type=MESH,
        )
        up = pltpu.make_async_remote_copy(
            src_ref=src, dst_ref=dst.at[0], send_sem=send.at[1], recv_sem=recv.at[0],
            device_id={"strip": jnp.minimum(s + 1, strip_n - 1)}, device_id_type=MESH,
        )

        @pl.when(below)
        def _():
            down.start()

        @pl.when(above)
        def _():
            up.start()

        def finish():
            @pl.when(below)
            def _():
                down.wait_send()
                up.wait_recv()

            @pl.when(above)
            def _():
                up.wait_send()
                down.wait_recv()

        return finish

    @pl.when(jnp.logical_not(below))
    def _():
        geo_in[0] = jnp.zeros(geo_in.shape[1:], jnp.float32)
        for k in range(SWEEPS + 1):
            field_in[k, 0] = jnp.zeros(field_in.shape[2:], jnp.float32)

    @pl.when(jnp.logical_not(above))
    def _():
        geo_in[1] = jnp.zeros(geo_in.shape[1:], jnp.float32)
        for k in range(SWEEPS + 1):
            field_in[k, 1] = jnp.zeros(field_in.shape[2:], jnp.float32)

    inv = 1.0 / (sigma * feature_scale)
    loads[0].wait()
    x = [tgt_pos[i : i + 1, :] for i in range(3)]
    xx = x[0] * x[0] + x[1] * x[1] + x[2] * x[2]
    one = jnp.ones((1, cands), jnp.float32)
    high, mid, low = split3(rows8(x + [xx * (-0.5 * inv), one], cands))
    tmat[2 * chans : 2 * chans + 48] = jnp.concatenate(
        [high, high, mid, mid, high, low], axis=0
    ).astype(jnp.bfloat16)
    high, mid, low = split3(rows8(x + [one], cands))
    columns = jnp.concatenate(
        [high, mid, low, jnp.zeros((LANES - 24, cands), jnp.float32)], axis=0
    )
    xmat[...] = jnp.transpose(columns).astype(jnp.bfloat16)
    for load in loads[1:5]:
        load.wait()

    first = f * half_tiles + c * own_tiles - 1
    for r in range(rows):
        tile = jnp.clip(first + r, 0, tiles - 1)
        span = pl.ds(pl.multiple_of(tile * LANES, LANES), LANES)
        here, moved, names = src_pos[:, span], disp[:, span], edges[:, span]
        for j in range(3):
            geo[j * rows + r : j * rows + r + 1, :] = here[j : j + 1]
            pos[j * rows + r : j * rows + r + 1, :] = moved[j : j + 1]
            edge[:, j * rows + r, :] = names
    rest = stack - 3 * rows
    geo[3 * rows :, :] = jnp.full((rest, LANES), count.astype(jnp.float32))
    pos[3 * rows :, :] = jnp.zeros((rest, LANES), jnp.float32)
    for k in range(edge_n):
        edge[k, 3 * rows :, :] = jnp.zeros((rest, LANES), jnp.int32)
    finish_geo = beside(geo, geo_in, geo_send, geo_recv)

    mine = wide_of(f)
    z = [src_pos[i : i + 1, mine] + disp[i : i + 1, mine] for i in range(3)]
    zz = z[0] * z[0] + z[1] * z[1] + z[2] * z[2]
    ones = jnp.ones((1, wide), jnp.float32)
    high, mid, low = split3(rows8([v * inv for v in z] + [ones, zz * (-0.5 * inv)], wide))
    saug[...] = jnp.concatenate([high, mid, high, mid, low, high], axis=0).astype(jnp.bfloat16)
    offset = c * cands
    state[0] = jnp.zeros((8, LANES), jnp.float32)
    state[half_tiles + 1] = jnp.zeros((8, LANES), jnp.float32)
    for load in loads[5:]:
        load.wait()
    for copy in feats:
        copy.wait()

    def block(tile, count_of):
        size = count_of * LANES
        span = pl.ds(pl.multiple_of(tile * LANES, LANES), size)
        lhs = jnp.concatenate([sfeat[:, span], saug[:, span]], axis=0)
        score = lax.dot_general(
            lhs, tmat[...], (((0,), (0,)), ((), ())), preferred_element_type=jnp.float32
        )
        seeds = []
        for i in range(count_of):
            row = seed[pl.ds(f * (half_tiles - 1) + tile + i, 1), :] - offset
            seeds.append(jnp.transpose(jnp.broadcast_to(row.astype(jnp.float32), (LANES, LANES))))
        seeds = jnp.concatenate(seeds, axis=0)
        lane = lax.broadcasted_iota(jnp.int32, (size, LANES), 1).astype(jnp.float32)
        pieces = []
        for t in range(cands // LANES):
            piece = score[:, t * LANES : (t + 1) * LANES]
            tie = jnp.where(seeds == lane + float(t * LANES), tie_gain / feature_scale, 0.0)
            pieces.append(piece + tie)
        best = pieces[0]
        for piece in pieces[1:]:
            best = jnp.maximum(best, piece)
        peak = jnp.maximum(jnp.max(best, axis=1, keepdims=True), FLOOR)
        weight = jnp.concatenate([jnp.exp2((piece - peak) * EXP2) for piece in pieces], axis=1)
        high = weight.astype(jnp.bfloat16)
        low = (weight - high.astype(jnp.float32)).astype(jnp.bfloat16)
        sums = jnp.dot(high, xmat[...], preferred_element_type=jnp.float32)
        sums = sums + jnp.dot(low, xmat[...], preferred_element_type=jnp.float32)
        at = lax.broadcasted_iota(jnp.int32, (size, LANES), 1)
        sums = jnp.where(at == 28, jnp.broadcast_to(peak, (size, LANES)), sums)
        for i in range(count_of):
            turned = jnp.transpose(sums[i * LANES : (i + 1) * LANES])
            state[other + tile + i] = turned[0:8] + turned[8:16] + turned[16:24] + turned[24:32]

    per = BLOCK // LANES

    def full(index, carry):
        block(index * per, per)
        return carry

    lax.fori_loop(0, (half_tiles + 1) // per, full, 0)
    if (half_tiles + 1) % per:
        block((half_tiles + 1) // per * per, (half_tiles + 1) % per)

    part_copies = []
    for dc in range(1, cand_n):
        to = lax.rem(c + dc, cand_n)
        copy = pltpu.make_async_remote_copy(
            src_ref=state.at[pl.ds(to * own_tiles, rows)], dst_ref=parts.at[c],
            send_sem=part_send.at[dc - 1], recv_sem=part_recv.at[dc - 1],
            device_id={"cand": to}, device_id_type=MESH,
        )
        copy.start()
        part_copies.append(copy)
    parts[c] = state[pl.ds(c * own_tiles, rows)]

    lane = lax.broadcasted_iota(jnp.int32, (stack, LANES), 1)
    row = lax.broadcasted_iota(jnp.int32, (stack, LANES), 0)
    coord = (row >= rows).astype(jnp.int32) + (row >= 2 * rows).astype(jnp.int32)
    row = first + row - coord * rows

    def pair(array):
        ends = jnp.where(lane < LANES // 2, pltpu.roll(array, stack - 1, 0), pltpu.roll(array, 1, 0))
        return array, ends

    def pick(arrays, at, inside):
        return jnp.where(
            inside,
            jnp.take_along_axis(arrays[0], at, axis=1, mode="promise_in_bounds"),
            jnp.take_along_axis(arrays[1], at, axis=1, mode="promise_in_bounds"),
        )

    def decode(k):
        e = edge[k]
        segment = (e >= points).astype(jnp.int32) + (e >= 2 * points).astype(jnp.int32)
        local = e - segment * points
        at = lax.bitwise_and(local, LANES - 1)
        return segment, local, at, lax.shift_right_logical(local, 7) == row

    slot = row * LANES + lane
    live = jnp.logical_and(jnp.logical_and(slot >= 0, slot < points), slot < count)
    finish_geo()
    counts = [geo_in[0, 3 * rows : 3 * rows + 1, :], geo[3 * rows : 3 * rows + 1, :],
              geo_in[1, 3 * rows : 3 * rows + 1, :]]
    sources = [pair(geo_in[0]), pair(geo[...]), pair(geo_in[1])]
    for k in range(edge_n):
        segment, local, at, inside = decode(k)
        near, limit = (
            jnp.where(segment == 1, b, jnp.where(segment == 0, a, d))
            for a, b, d in (
                [pick(source, at, inside) for source in sources],
                [jnp.broadcast_to(n, (stack, LANES)) for n in counts],
            )
        )
        step = jnp.where(coord == 0, strip_offset * (segment - 1).astype(jnp.float32), 0.0)
        gap = geo[...] - near - step
        gaps[k] = gap * gap
        weight = jnp.where(
            jnp.logical_and(live, local.astype(jnp.float32) < limit), 1.0 / edge_n, 0.0
        )
        kern_own[k] = jnp.where(segment == 1, weight, 0.0)
        kern_far[k] = jnp.where(segment == 1, 0.0, weight)
    for k in range(edge_n):
        squared = (
            gaps[k, 0:rows] + gaps[k, rows : 2 * rows] + gaps[k, 2 * rows : 3 * rows]
        )
        value = jnp.exp(squared * (-0.5 / kernel_scale))
        for j in range(3):
            gaps[k, j * rows : (j + 1) * rows] = value
        kern_own[k] = kern_own[k] * gaps[k]
        kern_far[k] = kern_far[k] * gaps[k]

    resid[...] = jnp.zeros((stack, LANES), jnp.float32)
    mass_s[...] = jnp.zeros((stack, LANES), jnp.float32)
    for copy in part_copies:
        copy.wait()
    peaks = [parts[i, :, 4, :] for i in range(cand_n)]
    peak = peaks[0]
    for one_peak in peaks[1:]:
        peak = jnp.maximum(peak, one_peak)
    sums = [jnp.zeros((rows, LANES), jnp.float32) for _ in range(4)]
    for i in range(cand_n):
        scale = jnp.exp2((peaks[i] - peak) * EXP2)
        sums = [sums[j] + parts[i, :, j, :] * scale for j in range(4)]
    denom = sums[3] + jnp.exp2((FLOOR - peak) * EXP2)
    on = live[0:rows].astype(jnp.float32)
    share = on / denom
    for j in range(3):
        resid[j * rows : (j + 1) * rows] = sums[j] * share
        mass_s[j * rows : (j + 1) * rows] = sums[3] * share
    mass = mass_s[...]
    resid[...] = resid[...] - mass * (geo[...] + pos[...])
    inverse = 1.0 / (mass + coherence * sigma)
    field[0] = resid[...] * inverse

    for step in range(SWEEPS + 1):
        finish = beside(field.at[step], field_in.at[step], field_send.at[step], field_recv.at[step])
        own = pair(field[step])
        acc = jnp.zeros((stack, LANES), jnp.float32)
        for k in range(edge_n):
            _, _, at, inside = decode(k)
            acc = acc + kern_own[k] * pick(own, at, inside)
        finish()
        low = pair(field_in[step, 0])
        high = pair(field_in[step, 1])
        for k in range(edge_n):
            segment, _, at, inside = decode(k)
            acc = acc + kern_far[k] * jnp.where(
                segment == 0, pick(low, at, inside), pick(high, at, inside)
            )
        if step < SWEEPS:
            field[step + 1] = (resid[...] - mass_s[...] * acc) * inverse
        else:
            pos[...] = pos[...] + field[step] + acc

    for r in range(own_tiles):
        span = pl.ds(pl.multiple_of((first + 1 + r) * LANES, LANES), LANES)
        for j in range(3):
            new_disp[j : j + 1, span] = pos[j * rows + r + 1 : j * rows + r + 2, :]
        mass_out[0:1, span] = mass_s[r + 1 : r + 2, :]
    span = pl.ds(pl.multiple_of((first + 1) * LANES, LANES), own_tiles * LANES)
    outs = []
    for i, (dc, df) in enumerate(peers):
        for j, ref in enumerate((new_disp, mass_out)):
            copy = pltpu.make_async_remote_copy(
                src_ref=ref.at[:, span], dst_ref=ref.at[:, span],
                send_sem=out_send.at[i, j], recv_sem=out_recv.at[i, j],
                device_id=peer(dc, df), device_id_type=MESH,
            )
            copy.start()
            outs.append(copy)
    for copy in outs:
        copy.wait()


def on_device(
    src_pos, src_feat, tgt_pos, tgt_feat, displacement, sigma_sq, seed_target, counts, edges
):
    chans, points = src_feat.shape
    cands = tgt_pos.shape[1]
    tiles = points // LANES
    wide = points // 2 + LANES
    edge_n = edges.shape[0]
    cand_n = lax.axis_size("cand")
    rows = tiles // (2 * cand_n) + 2
    assert REACH * (SWEEPS + 1) <= LANES
    grid = (-(-(3 * rows + 1) // 8) * 8, LANES)
    vmem = pl.BlockSpec(memory_space=pltpu.VMEM)
    smem = pl.BlockSpec(memory_space=pltpu.SMEM)
    hbm = pl.BlockSpec(memory_space=pltpu.HBM)
    f32, bf16, i32 = jnp.float32, jnp.bfloat16, jnp.int32
    dma = pltpu.SemaphoreType.DMA
    new_disp, mass = pl.pallas_call(
        cpd_kernel,
        out_shape=(
            jax.ShapeDtypeStruct((3, points), f32),
            jax.ShapeDtypeStruct((1, points), f32),
        ),
        in_specs=[smem, smem] + [hbm] * 7,
        out_specs=(vmem, vmem),
        scratch_shapes=[
            pltpu.VMEM((3, points), f32),
            pltpu.VMEM((3, points), f32),
            pltpu.VMEM((3, cands), f32),
            pltpu.VMEM((tiles, LANES), i32),
            pltpu.VMEM((edge_n, points), i32),
            pltpu.VMEM((2 * chans, wide), bf16),
            pltpu.VMEM((2 * chans + 48, cands), bf16),
            pltpu.VMEM((48, wide), bf16),
            pltpu.VMEM((cands, LANES), bf16),
            pltpu.VMEM((tiles // 2 + 2, 8, LANES), f32),
            pltpu.VMEM((cand_n, rows, 8, LANES), f32),
            pltpu.VMEM(grid, f32),
            pltpu.VMEM((edge_n,) + grid, i32),
            pltpu.VMEM(grid, f32),
            pltpu.VMEM((2,) + grid, f32),
            pltpu.VMEM((edge_n,) + grid, f32),
            pltpu.VMEM((edge_n,) + grid, f32),
            pltpu.VMEM((edge_n,) + grid, f32),
            pltpu.VMEM((SWEEPS + 1,) + grid, f32),
            pltpu.VMEM((SWEEPS + 1, 2) + grid, f32),
            pltpu.VMEM(grid, f32),
            pltpu.VMEM(grid, f32),
            dma((7,)),
            dma((2,)),
            dma((2,)),
            dma((cand_n,)),
            dma((cand_n,)),
            dma((2,)),
            dma((2,)),
            dma((SWEEPS + 1, 2)),
            dma((SWEEPS + 1, 2)),
            dma((2 * cand_n - 1, 2)),
            dma((2 * cand_n - 1, 2)),
        ],
        compiler_params=pltpu.CompilerParams(
            collective_id=0, has_side_effects=True, vmem_limit_bytes=48 << 20
        ),
    )(
        sigma_sq.reshape(1, 1), counts.reshape(1, 1), src_feat, tgt_feat, src_pos, displacement,
        tgt_pos, seed_target.reshape(tiles, LANES), edges,
    )
    return (new_disp, mass.reshape(points))


def solution(mesh):
    in_specs = (
        P(None, ("groups", "strip")),
        P("feat", ("groups", "strip")),
        P(None, ("groups", "strip", "cand")),
        P("feat", ("groups", "strip", "cand")),
        P(None, ("groups", "strip")),
        P(("groups", "strip")),
        P(("groups", "strip")),
        P(("groups", "strip")),
        P(None, ("groups", "strip")),
    )
    out_specs = (P(None, ("groups", "strip")), P(("groups", "strip")))
    return jax.shard_map(
        on_device, mesh=mesh, in_specs=in_specs, out_specs=out_specs, check_vma=False
    )
```

```python
import math

import jax
import jax.numpy as jnp
from jax import lax
from jax.experimental import pallas as pl
from jax.experimental.pallas import tpu as pltpu
from jax.sharding import PartitionSpec as P

SWEEPS = 4
LANES = 128
BLOCK = 256
REACH = 16

feature_scale = 0.18
tie_gain = 3.0
outlier_level = 1.0
strip_offset = 2.0
kernel_scale = 8.0
coherence = 0.1

EXP2 = feature_scale * math.log2(math.e)
FLOOR = outlier_level / feature_scale
MESH = pl.DeviceIdType.MESH


def split3(value):
    high = value.astype(jnp.bfloat16).astype(jnp.float32)
    rest = value - high
    mid = rest.astype(jnp.bfloat16).astype(jnp.float32)
    return high, mid, rest - mid


def rows8(rows, width):
    at = lax.broadcasted_iota(jnp.int32, (8, width), 0)
    out = jnp.zeros((8, width), jnp.float32)
    for i, row in enumerate(rows):
        out = jnp.where(at == i, jnp.broadcast_to(row, (8, width)), out)
    return out


def cpd_kernel(
    sigma_ref, count_ref, src_feat, tgt_feat, src_pos_in, disp_in, tgt_pos_in, seed_in, edges_in,
    new_disp, mass_out,
    src_pos, disp, tgt_pos, seed, edges, sfeat, tmat, saug, xmat, state,
    parts, pos, edge, geo, geo_in, gaps, kern_own, kern_far, field, field_in, resid, mass_s, whole, scores,
    local_sem, feat_send, feat_recv, part_send, part_recv, geo_send, geo_recv,
    field_send, field_recv, out_send, out_recv,
):
    chans, points = src_feat.shape
    cands = tgt_feat.shape[1]
    tiles = points // LANES
    half = points // 2
    half_tiles = tiles // 2
    wide = half + LANES
    cand_n, strip_n = lax.axis_size("cand"), lax.axis_size("strip")
    s, c, f = lax.axis_index("strip"), lax.axis_index("cand"), lax.axis_index("feat")
    other = 1 - f
    below, above = s > 0, s < strip_n - 1
    own_tiles = half_tiles // cand_n
    rows = own_tiles + 2
    stack = field.shape[1]
    edge_n = edges.shape[0]
    sigma = sigma_ref[0, 0]
    count = count_ref[0, 0]

    def wide_of(part):
        return pl.ds(pl.multiple_of(part * (half - LANES), LANES), wide)

    loads = [
        pltpu.make_async_copy(src, dst, local_sem.at[i])
        for i, (src, dst) in enumerate(
            [
                (tgt_pos_in, tgt_pos),
                (src_pos_in, src_pos),
                (disp_in, disp),
                (seed_in, seed),
                (edges_in, edges),
                (tgt_feat, tmat.at[pl.ds(0, chans)]),
                (src_feat.at[:, wide_of(f)], sfeat.at[pl.ds(0, chans)]),
            ]
        )
    ]
    for load in loads:
        load.start()

    barrier = pltpu.get_barrier_semaphore()
    peers = [(dc, df) for dc in range(cand_n) for df in range(2) if dc or df]

    def peer(dc, df):
        return {"cand": lax.rem(c + dc, cand_n), "feat": lax.rem(f + df, 2)}

    for dc, df in peers:
        pl.semaphore_signal(barrier, inc=1, device_id=peer(dc, df), device_id_type=MESH)

    @pl.when(below)
    def _():
        pl.semaphore_signal(barrier, inc=1, device_id={"strip": s - 1}, device_id_type=MESH)

    @pl.when(above)
    def _():
        pl.semaphore_signal(barrier, inc=1, device_id={"strip": s + 1}, device_id_type=MESH)

    pl.semaphore_wait(barrier, len(peers) + below.astype(jnp.int32) + above.astype(jnp.int32))

    feats = [
        pltpu.make_async_remote_copy(
            src_ref=src, dst_ref=dst, send_sem=feat_send.at[i], recv_sem=feat_recv.at[i],
            device_id={"feat": other}, device_id_type=MESH,
        )
        for i, (src, dst) in enumerate(
            [
                (tgt_feat, tmat.at[pl.ds(chans, chans)]),
                (src_feat.at[:, wide_of(other)], sfeat.at[pl.ds(chans, chans)]),
            ]
        )
    ]
    for copy in feats:
        copy.start()

    def beside(src, dst, send, recv):
        down = pltpu.make_async_remote_copy(
            src_ref=src, dst_ref=dst.at[1], send_sem=send.at[0], recv_sem=recv.at[1],
            device_id={"strip": jnp.maximum(s - 1, 0)}, device_id_type=MESH,
        )
        up = pltpu.make_async_remote_copy(
            src_ref=src, dst_ref=dst.at[0], send_sem=send.at[1], recv_sem=recv.at[0],
            device_id={"strip": jnp.minimum(s + 1, strip_n - 1)}, device_id_type=MESH,
        )

        @pl.when(below)
        def _():
            down.start()

        @pl.when(above)
        def _():
            up.start()

        def finish():
            @pl.when(below)
            def _():
                down.wait_send()
                up.wait_recv()

            @pl.when(above)
            def _():
                up.wait_send()
                down.wait_recv()

        return finish

    @pl.when(jnp.logical_not(below))
    def _():
        geo_in[0] = jnp.zeros(geo_in.shape[1:], jnp.float32)
        for k in range(SWEEPS + 1):
            field_in[k, 0] = jnp.zeros(field_in.shape[2:], jnp.float32)

    @pl.when(jnp.logical_not(above))
    def _():
        geo_in[1] = jnp.zeros(geo_in.shape[1:], jnp.float32)
        for k in range(SWEEPS + 1):
            field_in[k, 1] = jnp.zeros(field_in.shape[2:], jnp.float32)

    inv = 1.0 / (sigma * feature_scale)
    loads[0].wait()
    x = [tgt_pos[i : i + 1, :] for i in range(3)]
    xx = x[0] * x[0] + x[1] * x[1] + x[2] * x[2]
    one = jnp.ones((1, cands), jnp.float32)
    high, mid, low = split3(rows8(x + [xx * (-0.5 * inv), one], cands))
    tmat[2 * chans : 2 * chans + 48] = jnp.concatenate(
        [high, high, mid, mid, high, low], axis=0
    ).astype(jnp.bfloat16)
    high, mid, low = split3(rows8(x + [one], cands))
    columns = jnp.concatenate(
        [high, mid, low, jnp.zeros((LANES - 24, cands), jnp.float32)], axis=0
    )
    xmat[...] = jnp.transpose(columns).astype(jnp.bfloat16)
    for load in loads[1:5]:
        load.wait()

    first = f * half_tiles + c * own_tiles - 1
    for r in range(rows):
        tile = jnp.clip(first + r, 0, tiles - 1)
        span = pl.ds(pl.multiple_of(tile * LANES, LANES), LANES)
        here, moved, names = src_pos[:, span], disp[:, span], edges[:, span]
        for j in range(3):
            geo[j * rows + r : j * rows + r + 1, :] = here[j : j + 1]
            pos[j * rows + r : j * rows + r + 1, :] = moved[j : j + 1]
            edge[:, j * rows + r, :] = names
    rest = stack - 3 * rows
    geo[3 * rows :, :] = jnp.full((rest, LANES), count.astype(jnp.float32))
    pos[3 * rows :, :] = jnp.zeros((rest, LANES), jnp.float32)
    for k in range(edge_n):
        edge[k, 3 * rows :, :] = jnp.zeros((rest, LANES), jnp.int32)
    finish_geo = beside(geo, geo_in, geo_send, geo_recv)

    mine = wide_of(f)
    z = [src_pos[i : i + 1, mine] + disp[i : i + 1, mine] for i in range(3)]
    zz = z[0] * z[0] + z[1] * z[1] + z[2] * z[2]
    ones = jnp.ones((1, wide), jnp.float32)
    high, mid, low = split3(rows8([v * inv for v in z] + [ones, zz * (-0.5 * inv)], wide))
    saug[...] = jnp.concatenate([high, mid, high, mid, low, high], axis=0).astype(jnp.bfloat16)
    offset = c * cands
    state[0] = jnp.zeros((8, LANES), jnp.float32)
    state[half_tiles + 1] = jnp.zeros((8, LANES), jnp.float32)
    for load in loads[5:]:
        load.wait()
    for copy in feats:
        copy.wait()

    def products(tile, into):
        span = pl.ds(pl.multiple_of(tile * LANES, LANES), BLOCK)
        lhs = jnp.concatenate([sfeat[:, span], saug[:, span]], axis=0)
        scores[into] = lax.dot_general(
            lhs, tmat[...], (((0,), (0,)), ((), ())), preferred_element_type=jnp.float32
        )

    def block(tile, count_of, held):
        size = count_of * LANES
        seeds = []
        for i in range(count_of):
            row = seed[pl.ds(f * (half_tiles - 1) + tile + i, 1), :] - offset
            seeds.append(jnp.transpose(jnp.broadcast_to(row.astype(jnp.float32), (LANES, LANES))))
        seeds = jnp.concatenate(seeds, axis=0)
        lane = lax.broadcasted_iota(jnp.int32, (size, LANES), 1).astype(jnp.float32)
        pieces = []
        for t in range(cands // LANES):
            piece = scores[held, BLOCK - size :, t * LANES : (t + 1) * LANES]
            tie = jnp.where(seeds == lane + float(t * LANES), tie_gain / feature_scale, 0.0)
            pieces.append(piece + tie)
        best = pieces[0]
        for piece in pieces[1:]:
            best = jnp.maximum(best, piece)
        peak = jnp.maximum(jnp.max(best, axis=1, keepdims=True), FLOOR)
        weight = jnp.concatenate([jnp.exp2((piece - peak) * EXP2) for piece in pieces], axis=1)
        high = weight.astype(jnp.bfloat16)
        low = (weight - high.astype(jnp.float32)).astype(jnp.bfloat16)
        sums = jnp.dot(high, xmat[...], preferred_element_type=jnp.float32)
        sums = sums + jnp.dot(low, xmat[...], preferred_element_type=jnp.float32)
        at = lax.broadcasted_iota(jnp.int32, (size, LANES), 1)
        sums = jnp.where(at == 28, jnp.broadcast_to(peak, (size, LANES)), sums)
        for i in range(count_of):
            turned = jnp.transpose(sums[i * LANES : (i + 1) * LANES])
            state[other + tile + i] = turned[0:8] + turned[8:16] + turned[16:24] + turned[24:32]

    per = BLOCK // LANES

    last = half_tiles + 1 - per

    def full(index, carry):
        tile = index * 2 * per
        products(tile + per, 1)
        block(tile, per, 0)
        products(jnp.minimum(tile + 2 * per, last), 0)
        block(tile + per, per, 1)
        return carry

    assert half_tiles % (2 * per) == 0
    products(0, 0)
    lax.fori_loop(0, half_tiles // (2 * per), full, 0)
    block(half_tiles, 1, 0)

    part_copies = []
    for dc in range(1, cand_n):
        to = lax.rem(c + dc, cand_n)
        copy = pltpu.make_async_remote_copy(
            src_ref=state.at[pl.ds(to * own_tiles, rows)], dst_ref=parts.at[c],
            send_sem=part_send.at[dc - 1], recv_sem=part_recv.at[dc - 1],
            device_id={"cand": to}, device_id_type=MESH,
        )
        copy.start()
        part_copies.append(copy)
    parts[c] = state[pl.ds(c * own_tiles, rows)]

    lane = lax.broadcasted_iota(jnp.int32, (stack, LANES), 1)
    row = lax.broadcasted_iota(jnp.int32, (stack, LANES), 0)
    coord = (row >= rows).astype(jnp.int32) + (row >= 2 * rows).astype(jnp.int32)
    row = first + row - coord * rows

    def pair(array):
        ends = jnp.where(lane < LANES // 2, pltpu.roll(array, stack - 1, 0), pltpu.roll(array, 1, 0))
        return array, ends

    def pick(arrays, at, inside):
        return jnp.where(
            inside,
            jnp.take_along_axis(arrays[0], at, axis=1, mode="promise_in_bounds"),
            jnp.take_along_axis(arrays[1], at, axis=1, mode="promise_in_bounds"),
        )

    def decode(k):
        e = edge[k]
        segment = (e >= points).astype(jnp.int32) + (e >= 2 * points).astype(jnp.int32)
        local = e - segment * points
        at = lax.bitwise_and(local, LANES - 1)
        return segment, local, at, lax.shift_right_logical(local, 7) == row

    slot = row * LANES + lane
    live = jnp.logical_and(jnp.logical_and(slot >= 0, slot < points), slot < count)
    finish_geo()
    counts = [geo_in[0, 3 * rows : 3 * rows + 1, :], geo[3 * rows : 3 * rows + 1, :],
              geo_in[1, 3 * rows : 3 * rows + 1, :]]
    sources = [pair(geo_in[0]), pair(geo[...]), pair(geo_in[1])]
    for k in range(edge_n):
        segment, local, at, inside = decode(k)
        near, limit = (
            jnp.where(segment == 1, b, jnp.where(segment == 0, a, d))
            for a, b, d in (
                [pick(source, at, inside) for source in sources],
                [jnp.broadcast_to(n, (stack, LANES)) for n in counts],
            )
        )
        step = jnp.where(coord == 0, strip_offset * (segment - 1).astype(jnp.float32), 0.0)
        gap = geo[...] - near - step
        gaps[k] = gap * gap
        weight = jnp.where(
            jnp.logical_and(live, local.astype(jnp.float32) < limit), 1.0 / edge_n, 0.0
        )
        kern_own[k] = jnp.where(segment == 1, weight, 0.0)
        kern_far[k] = jnp.where(segment == 1, 0.0, weight)
    for k in range(edge_n):
        squared = (
            gaps[k, 0:rows] + gaps[k, rows : 2 * rows] + gaps[k, 2 * rows : 3 * rows]
        )
        value = jnp.exp(squared * (-0.5 / kernel_scale))
        for j in range(3):
            gaps[k, j * rows : (j + 1) * rows] = value
        kern_own[k] = kern_own[k] * gaps[k]
        kern_far[k] = kern_far[k] * gaps[k]

    resid[...] = jnp.zeros((stack, LANES), jnp.float32)
    mass_s[...] = jnp.zeros((stack, LANES), jnp.float32)
    for copy in part_copies:
        copy.wait()
    peaks = [parts[i, :, 4, :] for i in range(cand_n)]
    peak = peaks[0]
    for one_peak in peaks[1:]:
        peak = jnp.maximum(peak, one_peak)
    sums = [jnp.zeros((rows, LANES), jnp.float32) for _ in range(4)]
    for i in range(cand_n):
        scale = jnp.exp2((peaks[i] - peak) * EXP2)
        sums = [sums[j] + parts[i, :, j, :] * scale for j in range(4)]
    denom = sums[3] + jnp.exp2((FLOOR - peak) * EXP2)
    on = live[0:rows].astype(jnp.float32)
    share = on / denom
    for j in range(3):
        resid[j * rows : (j + 1) * rows] = sums[j] * share
        mass_s[j * rows : (j + 1) * rows] = sums[3] * share
    mass = mass_s[...]
    resid[...] = resid[...] - mass * (geo[...] + pos[...])
    inverse = 1.0 / (mass + coherence * sigma)
    field[0] = resid[...] * inverse

    for step in range(SWEEPS + 1):
        finish = beside(field.at[step], field_in.at[step], field_send.at[step], field_recv.at[step])
        own = pair(field[step])
        acc = jnp.zeros((stack, LANES), jnp.float32)
        for k in range(edge_n):
            _, _, at, inside = decode(k)
            acc = acc + kern_own[k] * pick(own, at, inside)
        finish()
        low = pair(field_in[step, 0])
        high = pair(field_in[step, 1])
        for k in range(edge_n):
            segment, _, at, inside = decode(k)
            acc = acc + kern_far[k] * jnp.where(
                segment == 0, pick(low, at, inside), pick(high, at, inside)
            )
        if step < SWEEPS:
            field[step + 1] = (resid[...] - mass_s[...] * acc) * inverse
        else:
            pos[...] = pos[...] + field[step] + acc

    for r in range(own_tiles):
        span = pl.ds(pl.multiple_of((first + 1 + r) * LANES, LANES), LANES)
        for j in range(3):
            whole[j : j + 1, span] = pos[j * rows + r + 1 : j * rows + r + 2, :]
        whole[3:4, span] = mass_s[r + 1 : r + 2, :]
    span = pl.ds(pl.multiple_of((first + 1) * LANES, LANES), own_tiles * LANES)
    outs = []
    for i, (dc, df) in enumerate(peers):
        copy = pltpu.make_async_remote_copy(
            src_ref=whole.at[:, span], dst_ref=whole.at[:, span],
            send_sem=out_send.at[i], recv_sem=out_recv.at[i],
            device_id=peer(dc, df), device_id_type=MESH,
        )
        copy.start()
        outs.append(copy)
    for copy in outs:
        copy.wait()
    new_disp[...] = whole[0:3]
    mass_out[...] = whole[3:4]


def on_device(
    src_pos, src_feat, tgt_pos, tgt_feat, displacement, sigma_sq, seed_target, counts, edges
):
    chans, points = src_feat.shape
    cands = tgt_pos.shape[1]
    tiles = points // LANES
    wide = points // 2 + LANES
    edge_n = edges.shape[0]
    cand_n = lax.axis_size("cand")
    rows = tiles // (2 * cand_n) + 2
    assert REACH * (SWEEPS + 1) <= LANES
    grid = (-(-(3 * rows + 1) // 8) * 8, LANES)
    vmem = pl.BlockSpec(memory_space=pltpu.VMEM)
    smem = pl.BlockSpec(memory_space=pltpu.SMEM)
    hbm = pl.BlockSpec(memory_space=pltpu.HBM)
    f32, bf16, i32 = jnp.float32, jnp.bfloat16, jnp.int32
    dma = pltpu.SemaphoreType.DMA
    new_disp, mass = pl.pallas_call(
        cpd_kernel,
        out_shape=(
            jax.ShapeDtypeStruct((3, points), f32),
            jax.ShapeDtypeStruct((1, points), f32),
        ),
        in_specs=[smem, smem] + [hbm] * 7,
        out_specs=(vmem, vmem),
        scratch_shapes=[
            pltpu.VMEM((3, points), f32),
            pltpu.VMEM((3, points), f32),
            pltpu.VMEM((3, cands), f32),
            pltpu.VMEM((tiles, LANES), i32),
            pltpu.VMEM((edge_n, points), i32),
            pltpu.VMEM((2 * chans, wide), bf16),
            pltpu.VMEM((2 * chans + 48, cands), bf16),
            pltpu.VMEM((48, wide), bf16),
            pltpu.VMEM((cands, LANES), bf16),
            pltpu.VMEM((tiles // 2 + 2, 8, LANES), f32),
            pltpu.VMEM((cand_n, rows, 8, LANES), f32),
            pltpu.VMEM(grid, f32),
            pltpu.VMEM((edge_n,) + grid, i32),
            pltpu.VMEM(grid, f32),
            pltpu.VMEM((2,) + grid, f32),
            pltpu.VMEM((edge_n,) + grid, f32),
            pltpu.VMEM((edge_n,) + grid, f32),
            pltpu.VMEM((edge_n,) + grid, f32),
            pltpu.VMEM((SWEEPS + 1,) + grid, f32),
            pltpu.VMEM((SWEEPS + 1, 2) + grid, f32),
            pltpu.VMEM(grid, f32),
            pltpu.VMEM(grid, f32),
            pltpu.VMEM((4, points), f32),
            pltpu.VMEM((2, BLOCK, cands), f32),
            dma((7,)),
            dma((2,)),
            dma((2,)),
            dma((cand_n,)),
            dma((cand_n,)),
            dma((2,)),
            dma((2,)),
            dma((SWEEPS + 1, 2)),
            dma((SWEEPS + 1, 2)),
            dma((2 * cand_n - 1,)),
            dma((2 * cand_n - 1,)),
        ],
        compiler_params=pltpu.CompilerParams(
            collective_id=0, has_side_effects=True, vmem_limit_bytes=63 << 20
        ),
    )(
        sigma_sq.reshape(1, 1), counts.reshape(1, 1), src_feat, tgt_feat, src_pos, displacement,
        tgt_pos, seed_target.reshape(tiles, LANES), edges,
    )
    return (new_disp, mass.reshape(points))


def solution(mesh):
    in_specs = (
        P(None, ("groups", "strip")),
        P("feat", ("groups", "strip")),
        P(None, ("groups", "strip", "cand")),
        P("feat", ("groups", "strip", "cand")),
        P(None, ("groups", "strip")),
        P(("groups", "strip")),
        P(("groups", "strip")),
        P(("groups", "strip")),
        P(None, ("groups", "strip")),
    )
    out_specs = (P(None, ("groups", "strip")), P(("groups", "strip")))
    return jax.shard_map(
        on_device, mesh=mesh, in_specs=in_specs, out_specs=out_specs, check_vma=False
    )
```

```python
import math

import jax
import jax.numpy as jnp
from jax import lax
from jax.experimental import pallas as pl
from jax.experimental.pallas import tpu as pltpu
from jax.sharding import PartitionSpec as P

SWEEPS = 4
LANES = 128
BLOCK = 256
REACH = 16

feature_scale = 0.18
tie_gain = 3.0
outlier_level = 1.0
strip_offset = 2.0
kernel_scale = 8.0
coherence = 0.1

EXP2 = feature_scale * math.log2(math.e)
FLOOR = outlier_level / feature_scale
MESH = pl.DeviceIdType.MESH


def split3(value):
    high = value.astype(jnp.bfloat16).astype(jnp.float32)
    rest = value - high
    mid = rest.astype(jnp.bfloat16).astype(jnp.float32)
    return high, mid, rest - mid


def rows8(rows, width):
    at = lax.broadcasted_iota(jnp.int32, (8, width), 0)
    out = jnp.zeros((8, width), jnp.float32)
    for i, row in enumerate(rows):
        out = jnp.where(at == i, jnp.broadcast_to(row, (8, width)), out)
    return out


def cpd_kernel(
    sigma_ref, count_ref, src_feat, tgt_feat, src_pos_in, disp_in, tgt_pos_in, seed_in, edges_in,
    new_disp, mass_out,
    src_pos, disp, tgt_pos, seed, edges, sfeat, tmat, saug, xmat, state,
    parts, pos, edge, geo, geo_in, gaps, kern_own, kern_far, field, field_in, resid, mass_s, whole, scores,
    local_sem, feat_send, feat_recv, part_send, part_recv, geo_send, geo_recv,
    field_send, field_recv, out_send, out_recv,
):
    chans, points = src_feat.shape
    cands = tgt_feat.shape[1]
    tiles = points // LANES
    half = points // 2
    half_tiles = tiles // 2
    wide = half + LANES
    cand_n, strip_n = lax.axis_size("cand"), lax.axis_size("strip")
    s, c, f = lax.axis_index("strip"), lax.axis_index("cand"), lax.axis_index("feat")
    other = 1 - f
    below, above = s > 0, s < strip_n - 1
    own_tiles = half_tiles // cand_n
    rows = own_tiles + 2
    stack = field.shape[1]
    edge_n = edges.shape[0]
    sigma = sigma_ref[0, 0]
    count = count_ref[0, 0]

    def wide_of(part):
        return pl.ds(pl.multiple_of(part * (half - LANES), LANES), wide)

    loads = [
        pltpu.make_async_copy(src, dst, local_sem.at[i])
        for i, (src, dst) in enumerate(
            [
                (tgt_pos_in, tgt_pos),
                (src_pos_in, src_pos),
                (disp_in, disp),
                (seed_in, seed),
                (edges_in, edges),
                (tgt_feat, tmat.at[pl.ds(0, chans)]),
                (src_feat.at[:, wide_of(f)], sfeat.at[pl.ds(0, chans)]),
            ]
        )
    ]
    for load in loads:
        load.start()

    barrier = pltpu.get_barrier_semaphore()
    peers = [(dc, df) for dc in range(cand_n) for df in range(2) if dc or df]

    def peer(dc, df):
        return {"cand": lax.rem(c + dc, cand_n), "feat": lax.rem(f + df, 2)}

    for dc, df in peers:
        pl.semaphore_signal(barrier, inc=1, device_id=peer(dc, df), device_id_type=MESH)

    @pl.when(below)
    def _():
        pl.semaphore_signal(barrier, inc=1, device_id={"strip": s - 1}, device_id_type=MESH)

    @pl.when(above)
    def _():
        pl.semaphore_signal(barrier, inc=1, device_id={"strip": s + 1}, device_id_type=MESH)

    pl.semaphore_wait(barrier, len(peers) + below.astype(jnp.int32) + above.astype(jnp.int32))

    feats = [
        pltpu.make_async_remote_copy(
            src_ref=src, dst_ref=dst, send_sem=feat_send.at[i], recv_sem=feat_recv.at[i],
            device_id={"feat": other}, device_id_type=MESH,
        )
        for i, (src, dst) in enumerate(
            [
                (tgt_feat, tmat.at[pl.ds(chans, chans)]),
                (src_feat.at[:, wide_of(other)], sfeat.at[pl.ds(chans, chans)]),
            ]
        )
    ]
    for copy in feats:
        copy.start()

    sent = []

    def beside(src, dst, send, recv):
        down = pltpu.make_async_remote_copy(
            src_ref=src, dst_ref=dst.at[1], send_sem=send.at[0], recv_sem=recv.at[1],
            device_id={"strip": jnp.maximum(s - 1, 0)}, device_id_type=MESH,
        )
        up = pltpu.make_async_remote_copy(
            src_ref=src, dst_ref=dst.at[0], send_sem=send.at[1], recv_sem=recv.at[0],
            device_id={"strip": jnp.minimum(s + 1, strip_n - 1)}, device_id_type=MESH,
        )

        @pl.when(below)
        def _():
            down.start()

        @pl.when(above)
        def _():
            up.start()

        def finish():
            @pl.when(below)
            def _():
                up.wait_recv()

            @pl.when(above)
            def _():
                down.wait_recv()

        sent.append((down, up))
        return finish

    @pl.when(jnp.logical_not(below))
    def _():
        geo_in[0] = jnp.zeros(geo_in.shape[1:], jnp.float32)
        for k in range(SWEEPS + 1):
            field_in[k, 0] = jnp.zeros(field_in.shape[2:], jnp.float32)

    @pl.when(jnp.logical_not(above))
    def _():
        geo_in[1] = jnp.zeros(geo_in.shape[1:], jnp.float32)
        for k in range(SWEEPS + 1):
            field_in[k, 1] = jnp.zeros(field_in.shape[2:], jnp.float32)

    inv = 1.0 / (sigma * feature_scale)
    loads[0].wait()
    x = [tgt_pos[i : i + 1, :] for i in range(3)]
    xx = x[0] * x[0] + x[1] * x[1] + x[2] * x[2]
    one = jnp.ones((1, cands), jnp.float32)
    high, mid, low = split3(rows8(x + [xx * (-0.5 * inv), one], cands))
    tmat[2 * chans : 2 * chans + 48] = jnp.concatenate(
        [high, high, mid, mid, high, low], axis=0
    ).astype(jnp.bfloat16)
    high, mid, low = split3(rows8(x + [one], cands))
    columns = jnp.concatenate(
        [high, mid, low, jnp.zeros((LANES - 24, cands), jnp.float32)], axis=0
    )
    xmat[...] = jnp.transpose(columns).astype(jnp.bfloat16)
    for load in loads[1:5]:
        load.wait()

    first = f * half_tiles + c * own_tiles - 1
    for r in range(rows):
        tile = jnp.clip(first + r, 0, tiles - 1)
        span = pl.ds(pl.multiple_of(tile * LANES, LANES), LANES)
        here, moved, names = src_pos[:, span], disp[:, span], edges[:, span]
        for j in range(3):
            geo[j * rows + r : j * rows + r + 1, :] = here[j : j + 1]
            pos[j * rows + r : j * rows + r + 1, :] = moved[j : j + 1]
            edge[:, j * rows + r, :] = names
    rest = stack - 3 * rows
    geo[3 * rows :, :] = jnp.full((rest, LANES), count.astype(jnp.float32))
    pos[3 * rows :, :] = jnp.zeros((rest, LANES), jnp.float32)
    for k in range(edge_n):
        edge[k, 3 * rows :, :] = jnp.zeros((rest, LANES), jnp.int32)
    finish_geo = beside(geo, geo_in, geo_send, geo_recv)

    mine = wide_of(f)
    z = [src_pos[i : i + 1, mine] + disp[i : i + 1, mine] for i in range(3)]
    zz = z[0] * z[0] + z[1] * z[1] + z[2] * z[2]
    ones = jnp.ones((1, wide), jnp.float32)
    high, mid, low = split3(rows8([v * inv for v in z] + [ones, zz * (-0.5 * inv)], wide))
    saug[...] = jnp.concatenate([high, mid, high, mid, low, high], axis=0).astype(jnp.bfloat16)
    offset = c * cands
    state[0] = jnp.zeros((8, LANES), jnp.float32)
    state[half_tiles + 1] = jnp.zeros((8, LANES), jnp.float32)
    for load in loads[5:]:
        load.wait()
    for copy in feats:
        copy.wait_recv()

    def products(tile, into):
        span = pl.ds(pl.multiple_of(tile * LANES, LANES), BLOCK)
        lhs = jnp.concatenate([sfeat[:, span], saug[:, span]], axis=0)
        scores[into] = lax.dot_general(
            lhs, tmat[...], (((0,), (0,)), ((), ())), preferred_element_type=jnp.float32
        )

    def block(tile, count_of, held):
        size = count_of * LANES
        seeds = []
        for i in range(count_of):
            row = seed[pl.ds(f * (half_tiles - 1) + tile + i, 1), :] - offset
            seeds.append(jnp.transpose(jnp.broadcast_to(row.astype(jnp.float32), (LANES, LANES))))
        seeds = jnp.concatenate(seeds, axis=0)
        lane = lax.broadcasted_iota(jnp.int32, (size, LANES), 1).astype(jnp.float32)
        pieces = []
        for t in range(cands // LANES):
            piece = scores[held, BLOCK - size :, t * LANES : (t + 1) * LANES]
            tie = jnp.where(seeds == lane + float(t * LANES), tie_gain / feature_scale, 0.0)
            pieces.append(piece + tie)
        best = pieces[0]
        for piece in pieces[1:]:
            best = jnp.maximum(best, piece)
        peak = jnp.maximum(jnp.max(best, axis=1, keepdims=True), FLOOR)
        weight = jnp.concatenate([jnp.exp2((piece - peak) * EXP2) for piece in pieces], axis=1)
        high = weight.astype(jnp.bfloat16)
        low = (weight - high.astype(jnp.float32)).astype(jnp.bfloat16)
        sums = jnp.dot(high, xmat[...], preferred_element_type=jnp.float32)
        sums = sums + jnp.dot(low, xmat[...], preferred_element_type=jnp.float32)
        at = lax.broadcasted_iota(jnp.int32, (size, LANES), 1)
        sums = jnp.where(at == 28, jnp.broadcast_to(peak, (size, LANES)), sums)
        for i in range(count_of):
            turned = jnp.transpose(sums[i * LANES : (i + 1) * LANES])
            state[other + tile + i] = turned[0:8] + turned[8:16] + turned[16:24] + turned[24:32]

    per = BLOCK // LANES

    last = half_tiles + 1 - per

    def full(index, carry):
        tile = index * 2 * per
        products(tile + per, 1)
        block(tile, per, 0)
        products(jnp.minimum(tile + 2 * per, last), 0)
        block(tile + per, per, 1)
        return carry

    assert half_tiles % (2 * per) == 0
    products(0, 0)
    lax.fori_loop(0, half_tiles // (2 * per), full, 0)
    block(half_tiles, 1, 0)

    part_copies = []
    for dc in range(1, cand_n):
        to = lax.rem(c + dc, cand_n)
        copy = pltpu.make_async_remote_copy(
            src_ref=state.at[pl.ds(to * own_tiles, rows)], dst_ref=parts.at[c],
            send_sem=part_send.at[dc - 1], recv_sem=part_recv.at[dc - 1],
            device_id={"cand": to}, device_id_type=MESH,
        )
        copy.start()
        part_copies.append(copy)
    parts[c] = state[pl.ds(c * own_tiles, rows)]

    lane = lax.broadcasted_iota(jnp.int32, (stack, LANES), 1)
    row = lax.broadcasted_iota(jnp.int32, (stack, LANES), 0)
    coord = (row >= rows).astype(jnp.int32) + (row >= 2 * rows).astype(jnp.int32)
    row = first + row - coord * rows

    def pair(array):
        ends = jnp.where(lane < LANES // 2, pltpu.roll(array, stack - 1, 0), pltpu.roll(array, 1, 0))
        return array, ends

    def pick(arrays, at, inside):
        return jnp.where(
            inside,
            jnp.take_along_axis(arrays[0], at, axis=1, mode="promise_in_bounds"),
            jnp.take_along_axis(arrays[1], at, axis=1, mode="promise_in_bounds"),
        )

    def decode(k):
        e = edge[k]
        segment = (e >= points).astype(jnp.int32) + (e >= 2 * points).astype(jnp.int32)
        local = e - segment * points
        at = lax.bitwise_and(local, LANES - 1)
        return segment, local, at, lax.shift_right_logical(local, 7) == row

    slot = row * LANES + lane
    live = jnp.logical_and(jnp.logical_and(slot >= 0, slot < points), slot < count)
    finish_geo()
    counts = [geo_in[0, 3 * rows : 3 * rows + 1, :], geo[3 * rows : 3 * rows + 1, :],
              geo_in[1, 3 * rows : 3 * rows + 1, :]]
    sources = [pair(geo_in[0]), pair(geo[...]), pair(geo_in[1])]
    for k in range(edge_n):
        segment, local, at, inside = decode(k)
        near, limit = (
            jnp.where(segment == 1, b, jnp.where(segment == 0, a, d))
            for a, b, d in (
                [pick(source, at, inside) for source in sources],
                [jnp.broadcast_to(n, (stack, LANES)) for n in counts],
            )
        )
        step = jnp.where(coord == 0, strip_offset * (segment - 1).astype(jnp.float32), 0.0)
        gap = geo[...] - near - step
        gaps[k] = gap * gap
        weight = jnp.where(
            jnp.logical_and(live, local.astype(jnp.float32) < limit), 1.0 / edge_n, 0.0
        )
        kern_own[k] = jnp.where(segment == 1, weight, 0.0)
        kern_far[k] = jnp.where(segment == 1, 0.0, weight)
    for k in range(edge_n):
        squared = (
            gaps[k, 0:rows] + gaps[k, rows : 2 * rows] + gaps[k, 2 * rows : 3 * rows]
        )
        value = jnp.exp(squared * (-0.5 / kernel_scale))
        for j in range(3):
            gaps[k, j * rows : (j + 1) * rows] = value
        kern_own[k] = kern_own[k] * gaps[k]
        kern_far[k] = kern_far[k] * gaps[k]

    resid[...] = jnp.zeros((stack, LANES), jnp.float32)
    mass_s[...] = jnp.zeros((stack, LANES), jnp.float32)
    for copy in part_copies:
        copy.wait_recv()
    peaks = [parts[i, :, 4, :] for i in range(cand_n)]
    peak = peaks[0]
    for one_peak in peaks[1:]:
        peak = jnp.maximum(peak, one_peak)
    sums = [jnp.zeros((rows, LANES), jnp.float32) for _ in range(4)]
    for i in range(cand_n):
        scale = jnp.exp2((peaks[i] - peak) * EXP2)
        sums = [sums[j] + parts[i, :, j, :] * scale for j in range(4)]
    denom = sums[3] + jnp.exp2((FLOOR - peak) * EXP2)
    on = live[0:rows].astype(jnp.float32)
    share = on / denom
    for j in range(3):
        resid[j * rows : (j + 1) * rows] = sums[j] * share
        mass_s[j * rows : (j + 1) * rows] = sums[3] * share
    mass = mass_s[...]
    resid[...] = resid[...] - mass * (geo[...] + pos[...])
    inverse = 1.0 / (mass + coherence * sigma)
    field[0] = resid[...] * inverse

    for step in range(SWEEPS + 1):
        finish = beside(field.at[step], field_in.at[step], field_send.at[step], field_recv.at[step])
        own = pair(field[step])
        acc = jnp.zeros((stack, LANES), jnp.float32)
        for k in range(edge_n):
            _, _, at, inside = decode(k)
            acc = acc + kern_own[k] * pick(own, at, inside)
        finish()
        low = pair(field_in[step, 0])
        high = pair(field_in[step, 1])
        for k in range(edge_n):
            segment, _, at, inside = decode(k)
            acc = acc + kern_far[k] * jnp.where(
                segment == 0, pick(low, at, inside), pick(high, at, inside)
            )
        if step < SWEEPS:
            field[step + 1] = (resid[...] - mass_s[...] * acc) * inverse
        else:
            pos[...] = pos[...] + field[step] + acc

    for r in range(own_tiles):
        span = pl.ds(pl.multiple_of((first + 1 + r) * LANES, LANES), LANES)
        for j in range(3):
            whole[j : j + 1, span] = pos[j * rows + r + 1 : j * rows + r + 2, :]
        whole[3:4, span] = mass_s[r + 1 : r + 2, :]
    span = pl.ds(pl.multiple_of((first + 1) * LANES, LANES), own_tiles * LANES)
    outs = []
    for i, (dc, df) in enumerate(peers):
        copy = pltpu.make_async_remote_copy(
            src_ref=whole.at[:, span], dst_ref=whole.at[:, span],
            send_sem=out_send.at[i], recv_sem=out_recv.at[i],
            device_id=peer(dc, df), device_id_type=MESH,
        )
        copy.start()
        outs.append(copy)
    for copy in feats + part_copies:
        copy.wait_send()

    @pl.when(below)
    def _():
        for down, up in sent:
            down.wait_send()

    @pl.when(above)
    def _():
        for down, up in sent:
            up.wait_send()

    for copy in outs:
        copy.wait()
    new_disp[...] = whole[0:3]
    mass_out[...] = whole[3:4]


def on_device(
    src_pos, src_feat, tgt_pos, tgt_feat, displacement, sigma_sq, seed_target, counts, edges
):
    chans, points = src_feat.shape
    cands = tgt_pos.shape[1]
    tiles = points // LANES
    wide = points // 2 + LANES
    edge_n = edges.shape[0]
    cand_n = lax.axis_size("cand")
    rows = tiles // (2 * cand_n) + 2
    assert REACH * (SWEEPS + 1) <= LANES
    grid = (-(-(3 * rows + 1) // 8) * 8, LANES)
    vmem = pl.BlockSpec(memory_space=pltpu.VMEM)
    smem = pl.BlockSpec(memory_space=pltpu.SMEM)
    hbm = pl.BlockSpec(memory_space=pltpu.HBM)
    f32, bf16, i32 = jnp.float32, jnp.bfloat16, jnp.int32
    dma = pltpu.SemaphoreType.DMA
    new_disp, mass = pl.pallas_call(
        cpd_kernel,
        out_shape=(
            jax.ShapeDtypeStruct((3, points), f32),
            jax.ShapeDtypeStruct((1, points), f32),
        ),
        in_specs=[smem, smem] + [hbm] * 7,
        out_specs=(vmem, vmem),
        scratch_shapes=[
            pltpu.VMEM((3, points), f32),
            pltpu.VMEM((3, points), f32),
            pltpu.VMEM((3, cands), f32),
            pltpu.VMEM((tiles, LANES), i32),
            pltpu.VMEM((edge_n, points), i32),
            pltpu.VMEM((2 * chans, wide), bf16),
            pltpu.VMEM((2 * chans + 48, cands), bf16),
            pltpu.VMEM((48, wide), bf16),
            pltpu.VMEM((cands, LANES), bf16),
            pltpu.VMEM((tiles // 2 + 2, 8, LANES), f32),
            pltpu.VMEM((cand_n, rows, 8, LANES), f32),
            pltpu.VMEM(grid, f32),
            pltpu.VMEM((edge_n,) + grid, i32),
            pltpu.VMEM(grid, f32),
            pltpu.VMEM((2,) + grid, f32),
            pltpu.VMEM((edge_n,) + grid, f32),
            pltpu.VMEM((edge_n,) + grid, f32),
            pltpu.VMEM((edge_n,) + grid, f32),
            pltpu.VMEM((SWEEPS + 1,) + grid, f32),
            pltpu.VMEM((SWEEPS + 1, 2) + grid, f32),
            pltpu.VMEM(grid, f32),
            pltpu.VMEM(grid, f32),
            pltpu.VMEM((4, points), f32),
            pltpu.VMEM((2, BLOCK, cands), f32),
            dma((7,)),
            dma((2,)),
            dma((2,)),
            dma((cand_n,)),
            dma((cand_n,)),
            dma((2,)),
            dma((2,)),
            dma((SWEEPS + 1, 2)),
            dma((SWEEPS + 1, 2)),
            dma((2 * cand_n - 1,)),
            dma((2 * cand_n - 1,)),
        ],
        compiler_params=pltpu.CompilerParams(
            collective_id=0, has_side_effects=True, vmem_limit_bytes=63 << 20
        ),
    )(
        sigma_sq.reshape(1, 1), counts.reshape(1, 1), src_feat, tgt_feat, src_pos, displacement,
        tgt_pos, seed_target.reshape(tiles, LANES), edges,
    )
    return (new_disp, mass.reshape(points))


def solution(mesh):
    in_specs = (
        P(None, ("groups", "strip")),
        P("feat", ("groups", "strip")),
        P(None, ("groups", "strip", "cand")),
        P("feat", ("groups", "strip", "cand")),
        P(None, ("groups", "strip")),
        P(("groups", "strip")),
        P(("groups", "strip")),
        P(("groups", "strip")),
        P(None, ("groups", "strip")),
    )
    out_specs = (P(None, ("groups", "strip")), P(("groups", "strip")))
    return jax.shard_map(
        on_device, mesh=mesh, in_specs=in_specs, out_specs=out_specs, check_vma=False
    )
```
